32 devices in a mesh: dom: 8 (over z, x), bud: 4 (over y, core).
Axes of the slice: x: 2, y: 2, z: 4, core: 2. Of those that a mesh axis runs over, the one named last changes fastest.
Arguments:
- right_side: float32 [3, 32, 64, 128], P(None, 'dom', 'bud'), may hold values from -8 to 8
- stiffness: float32 [32, 64, 128], P('dom', 'bud'), may hold values from 0.5 to 2
- coupling: float32 [27, 3, 3], replicated, may hold values from -2 to 3, as said below
- iterate_in: float32 [3, 32, 64, 128], P(None, 'dom', 'bud'), may hold values from -8 to 8
- residual_in: float32 [3, 32, 64, 128], P(None, 'dom', 'bud'), may hold values from -20 to 20
- direction_in: float32 [3, 32, 64, 128], P(None, 'dom', 'bud'), may hold values from -20 to 20
- backup_in: float32 [2, 3, 32, 64, 128], P(None, None, 'dom', 'bud'), may hold values from -8 to 8
- beta_prev: float32 [1], replicated, may hold values from 0.3 to 0.9
- fail_column: int32 [8], P('dom'), may hold values from 0 to 3, as said below
- buddy_bit: int32 [8], P('dom'), may hold values from 0 to 1
Outputs:
- iterate: float32 [3, 32, 64, 128], P(None, 'dom', 'bud')
- residual: float32 [3, 32, 64, 128], P(None, 'dom', 'bud')
- backup: float32 [2, 3, 32, 64, 128], P(None, None, 'dom', 'bud')
The draws below stay inside these ranges and needn't reach their ends.
Inputs may be any that keep to these rules, and one draw needn't show every extreme that they name: `fail_column`: every column index appears among the lost columns. The buddy of block (i, k) is the block (i, k with binary digit buddy_bit[i] flipped). coupling[26 - o] is the transpose of coupling[o]; each diagonal entry of coupling[13] exceeds 1.02 times the sum of the magnitudes of all other entries of its row over all 27 blocks.
All inputs are finite; a program needn't handle non-finite values.
Results may differ from the reference program's by a relative error of at most 0.00015.
Values sent between devices are 32-bit elements; how exact they have to be, the bound alone decides.
A program may use at most 64 MiB of HBM per device.

```python
import math
import jax
import jax.numpy as jnp
import numpy as np
from jax import lax

CX = 4
CY = 16
SWEEPS = 4
NX = 32
NY = 64
NZ = 128
BLOCK_ROWS = 8
LEVELS = 2
N_DOM = 8
N_BUD = 4


def draw_fail_column(key, part):
    order = jax.random.permutation(jax.random.fold_in(key, 3), jnp.arange(BLOCK_ROWS, dtype=jnp.int32))
    return (order % N_BUD).astype(jnp.int32)


def draw_residual_in(key, part):
    random_part = jax.random.normal(jax.random.fold_in(key, 5), (3, NX, NY, NZ), jnp.float32)
    position = jnp.arange(NX, dtype=jnp.float32) / NX
    rising = 1.0 + 2.0 * position
    return jnp.clip(random_part * rising[None, :, None, None], -20.0, 20.0)


def draw_direction_in(key, part):
    random_part = jax.random.normal(jax.random.fold_in(key, 25), (3, NX, NY, NZ), jnp.float32)
    position = jnp.arange(NX, dtype=jnp.float32) / NX
    rising = 1.0 + 2.0 * position
    return jnp.clip(random_part * rising[None, :, None, None], -20.0, 20.0)


def draw_coupling(key, part):
    first_key, second_key, third_key = jax.random.split(jax.random.fold_in(key, 17), 3)
    identity = jnp.eye(3, dtype=jnp.float32)
    spread = jax.random.normal(first_key, (27, 3, 3), jnp.float32) * 0.25
    strength = jax.random.uniform(second_key, (27, 3), jnp.float32, 0.5, 1.5)
    drawn = spread * (1.0 - identity)[None] - strength[:, :, None] * identity[None]
    mirrored = 0.5 * (drawn + jnp.transpose(drawn[::-1], (0, 2, 1)))
    middle = jax.random.normal(third_key, (3, 3), jnp.float32) * 0.3
    middle = 0.5 * (middle + middle.T) * (1.0 - identity)
    outer_abs = jnp.sum(jnp.abs(mirrored), axis=(0, 2)) - jnp.sum(jnp.abs(mirrored[13]), axis=1)
    row_total = outer_abs + jnp.sum(jnp.abs(middle), axis=1)
    center_block = middle + identity * (1.02 * row_total)[:, None]
    coupled = mirrored.at[13].set(center_block)
    return coupled / jnp.mean(1.02 * row_total)


def with_ends(array, rng, least, top_value):
    longest = array.shape.index(max(array.shape))
    spots = []
    for shift in (0, 1):
        where = [jax.random.randint(jax.random.fold_in(rng, axis), (), 0, length) for axis, length in enumerate(array.shape)]
        where[longest] = (where[longest] + shift) % array.shape[longest]
        spots.append(tuple(where))
    return array.at[spots[0]].set(least).at[spots[1]].set(top_value)


def levels(rng, shape, cuts, low, top_value):
    def one(dim, blocks):
        heights = jax.random.uniform(jax.random.fold_in(jax.random.fold_in(rng, 6), dim), (blocks,), jnp.float32, low / len(cuts), top_value / len(cuts))
        return jnp.repeat(jnp.exp(heights), shape[dim] // blocks).reshape((-1,) + (1,) * (len(shape) - dim - 1))

    factor_of = one(*cuts[0])
    for cut in cuts[1:]:
        factor_of = factor_of * one(*cut)
    return factor_of


def centred(own_key, shape, scale, most, cuts=(), kind=jnp.bfloat16):
    array = scale * jax.random.normal(own_key, shape, jnp.float32)
    if cuts:
        array = array * levels(own_key, shape, cuts, -0.22, 0.18)
    return jnp.clip(array, -most, most).astype(kind)


def setup_inputs(seed: int = 0) -> dict:
    splits = jax.random.split(jax.random.key(seed), 11)
    right_side = centred(splits[0], (3, NX, NY, NZ), 1.0, 8.0, ((1, 8), (2, 4)), jnp.float32)
    stiffness = jnp.clip(jnp.exp(math.log(2.0) - 1.3862944 * jax.random.uniform(splits[1], (NX, NY, NZ), jnp.float32) ** levels(splits[1], (NX, NY, NZ), ((0, 8), (1, 4)), -0.2, 0.2)), 0.5, 2.0)
    coupling = draw_coupling(jax.random.fold_in(splits[10], 71), 0)
    iterate_in = centred(splits[3], (3, NX, NY, NZ), 1.0, 8.0, ((1, 8), (2, 4)), jnp.float32)
    residual_in = draw_residual_in(jax.random.fold_in(splits[10], 71), 0)
    direction_in = draw_direction_in(jax.random.fold_in(splits[10], 71), 0)
    backup_in = centred(splits[6], (2, 3, NX, NY, NZ), 1.0, 8.0, ((2, 8), (3, 4)), jnp.float32)
    beta_prev = jnp.clip(jax.random.uniform(splits[7], (1,), jnp.float32, 0.3, 0.9), 0.3, 0.9)
    fail_column = draw_fail_column(jax.random.fold_in(splits[10], 71), 0)
    buddy_bit = with_ends(jax.random.randint(splits[9], (BLOCK_ROWS,), 0, LEVELS), jax.random.fold_in(splits[9], 1), 0, LEVELS - 1).astype(jnp.int32)
    return dict(right_side=right_side, stiffness=stiffness, coupling=coupling, iterate_in=iterate_in, residual_in=residual_in, direction_in=direction_in, backup_in=backup_in, beta_prev=beta_prev, fail_column=fail_column, buddy_bit=buddy_bit)


LOW = 0.01
HIGH = 1.99


def stencil(padded, coupling):
    size_x = padded.shape[1] - 2
    size_y = padded.shape[2] - 2
    size_z = padded.shape[3] - 2
    summed = jnp.zeros((3, size_x, size_y, size_z), padded.dtype)
    for offset in range(27):
        shift_x = offset // 9
        shift_y = (offset // 3) % 3
        shift_z = offset % 3
        window = padded[:, shift_x:shift_x + size_x, shift_y:shift_y + size_y, shift_z:shift_z + size_z]
        summed = summed + jnp.einsum("ab,bxyz->axyz", coupling[offset], window, precision=lax.Precision.HIGHEST)
    return summed


def operate(vector, stiffness, coupling):
    scaled = vector * stiffness[None]
    padded = jnp.pad(scaled, ((0, 0), (1, 1), (1, 1), (1, 1)))
    return stencil(padded, coupling) * stiffness[None]


def pick_blocks(field, columns):
    shaped = field.reshape(3, N_DOM, CX, N_BUD, CY, NZ)
    picked = jnp.take_along_axis(shaped, columns[None, :, None, None, None, None], axis=3)[:, :, :, 0]
    return jnp.moveaxis(picked, 1, 0)


def place_blocks(blocks, base, lost_cells):
    spread = jnp.moveaxis(blocks, 0, 1)[:, :, :, None]
    spread = jnp.broadcast_to(spread, (3, N_DOM, CX, N_BUD, CY, NZ)).reshape(3, NX, NY, NZ)
    return jnp.where(lost_cells[None, :, :, None], spread, base)


def reference(right_side, stiffness, coupling, iterate_in, residual_in, direction_in, backup_in, beta_prev, fail_column, buddy_bit):
    center = jnp.diagonal(coupling[13])
    diagonal = stiffness[None] ** 2 * center[:, None, None, None]
    inverse = 1.0 / diagonal

    columns = fail_column.astype(jnp.int32)
    stride = jnp.left_shift(jnp.ones_like(columns), buddy_bit.astype(jnp.int32))
    buddy_columns = (columns + stride * (1 - 2 * ((columns // stride) % 2))).astype(jnp.int32)
    lost_rows = columns[:, None] == jnp.arange(N_BUD, dtype=jnp.int32)[None, :]
    lost_cells = jnp.broadcast_to(lost_rows[:, None, :, None], (N_DOM, CX, N_BUD, CY)).reshape(NX, NY)

    saved_prev = pick_blocks(backup_in[0], buddy_columns)
    saved_dir = pick_blocks(backup_in[1], buddy_columns)
    right_blocks = pick_blocks(right_side, columns)
    stiff_shaped = stiffness.reshape(N_DOM, CX, N_BUD, CY, NZ)
    stiff_blocks = jnp.take_along_axis(stiff_shaped, columns[:, None, None, None, None], axis=2)[:, :, 0]

    zeroed = jnp.where(lost_cells[None, :, :, None], 0.0, iterate_in)
    outside_all = operate(zeroed, stiffness, coupling)
    outer_blocks = pick_blocks(outside_all, columns)

    def rebuild_one(right_block, stiff_block, prev_block, dir_block, outer_term):
        diag_block = stiff_block[None] ** 2 * center[:, None, None, None]
        inverse_block = 1.0 / diag_block
        restored_z = dir_block - beta_prev[0] * prev_block
        restored_r = diag_block * restored_z
        target = right_block - restored_r - outer_term
        centre_value = (HIGH + LOW) / 2.0
        half_width = (HIGH - LOW) / 2.0
        ratio_value = centre_value / half_width
        recursion_weight = 1.0 / ratio_value
        update = inverse_block * target / centre_value
        solved = jnp.zeros_like(target)
        for sweep in range(SWEEPS):
            solved = solved + update
            if sweep < SWEEPS - 1:
                remain = target - operate(solved, stiff_block, coupling)
                weight_next = 1.0 / (2.0 * ratio_value - recursion_weight)
                update = weight_next * recursion_weight * update + (2.0 * weight_next / half_width) * inverse_block * remain
                recursion_weight = weight_next
        return solved, restored_r

    solved_blocks, restored_blocks = jax.vmap(rebuild_one)(right_blocks, stiff_blocks, saved_prev, saved_dir, outer_blocks)

    start_iter = place_blocks(solved_blocks, iterate_in, lost_cells)
    residual = place_blocks(restored_blocks, residual_in, lost_cells)
    direction = place_blocks(saved_dir, direction_in, lost_cells)

    preconditioned = inverse * residual
    norm_first = jnp.sum(residual * preconditioned)
    product_image = operate(direction, stiffness, coupling)
    alpha_first = norm_first / jnp.sum(direction * product_image)
    iterate_mid = start_iter + alpha_first * direction
    residual = residual - alpha_first * product_image
    preconditioned = inverse * residual
    norm_second = jnp.sum(residual * preconditioned)
    beta_first = norm_second / norm_first
    second_dir = preconditioned + beta_first * direction
    product_image = operate(second_dir, stiffness, coupling)
    alpha_second = norm_second / jnp.sum(second_dir * product_image)
    final_iterate = iterate_mid + alpha_second * second_dir
    final_residual = residual - alpha_second * product_image

    stacked = jnp.stack([direction, second_dir])
    blocks = stacked.reshape(2, 3, N_DOM, CX, N_BUD, CY, NZ)
    column_ids = np.arange(N_BUD)
    backup_blocks = jnp.zeros_like(blocks)
    for bit_level in range(LEVELS):
        level_stride = 2 ** bit_level
        partner = column_ids + level_stride * (1 - 2 * ((column_ids // level_stride) % 2))
        candidate = blocks[:, :, :, :, partner]
        chosen = (buddy_bit == bit_level)[None, None, :, None, None, None, None]
        backup_blocks = jnp.where(chosen, candidate, backup_blocks)
    backup = backup_blocks.reshape(2, 3, NX, NY, NZ)
    return (final_iterate, final_residual, backup)
```

```python
import functools

import jax
import jax.numpy as jnp
from jax import lax
from jax.experimental import pallas as pl
from jax.experimental.pallas import tpu as pltpu
from jax.sharding import PartitionSpec as P

SWEEPS = 4
LOW = 0.01
HIGH = 1.99
SIDES = [(sx, sy) for sx in (-1, 0, 1) for sy in (-1, 0, 1) if (sx, sy) != (0, 0)]
Y0 = 8


def kernel(
    nd, nb, levels,
    rhs, stiff, cpl, x_in, r_in, p_in, bk, beta, fc, bb,
    x_out, r_out, b_out,
    pads, padl, flat, ysend, yrecv, csend, crecv, saved, bsend, brecv,
    r0, inv, img, target, solved, update,
    red, red2, rrecv, brecv2,
    hs, hr, ss, sr, bs, br, d1s, d1r, d2s, d2r,
):
    nx, ny, nz = stiff.shape
    step = 2 if nx % 2 == 0 else 1
    dom, bud = lax.axis_index("dom"), lax.axis_index("bud")

    def has(side):
        sx, sy = side
        ok = None
        for cond in (
            ([dom > 0] if sx < 0 else [dom < nd - 1] if sx > 0 else [])
            + ([bud > 0] if sy < 0 else [bud < nb - 1] if sy > 0 else [])
        ):
            ok = cond if ok is None else jnp.logical_and(ok, cond)
        return ok

    def remote(src, dst, send, recv, d, b):
        return pltpu.make_async_remote_copy(
            src_ref=src, dst_ref=dst, send_sem=send, recv_sem=recv,
            device_id={"dom": d, "bud": b}, device_id_type=pl.DeviceIdType.MESH,
        )

    def flip(level):
        stride = 1 << level
        return bud + stride * (1 - 2 * (lax.rem(bud // stride, 2)))

    pads[...] = jnp.zeros(pads.shape, pads.dtype)
    padl[...] = jnp.zeros(padl.shape, padl.dtype)
    yrecv[...] = jnp.zeros(yrecv.shape, yrecv.dtype)
    crecv[...] = jnp.zeros(crecv.shape, crecv.dtype)

    barrier = pltpu.get_barrier_semaphore()

    def greet(d, b):
        pl.semaphore_signal(
            barrier, inc=1, device_id={"dom": d, "bud": b},
            device_id_type=pl.DeviceIdType.MESH,
        )

    for j in range(1, nb):
        greet(dom, lax.rem(bud + j, nb))
    for j in range(1, nd):
        greet(lax.rem(dom + j, nd), bud)
    diagonals = [s for s in SIDES if s[0] != 0 and s[1] != 0]
    for side in diagonals:
        @pl.when(has(side))
        def _(side=side):
            greet(dom + side[0], bud + side[1])

    me_failed = jnp.full((1, ny, nz), fc[0], jnp.int32) == bud
    bit_here = jnp.full((1, ny, nz), bb[0], jnp.int32)

    def halo_copies(e, which, side):
        sx, sy = side
        i = SIDES.index(side)
        o = SIDES.index((-sx, -sy))
        to = (dom + sx, bud + sy)
        if sy == 0:
            src = flat.at[e, :, nx - 1 if sx > 0 else 0]
            dst = pads.at[e, :, 0 if sx > 0 else nx + 1, pl.ds(Y0, ny), :]
        elif sx == 0:
            src = ysend.at[e, 1 if sy > 0 else 0]
            dst = yrecv.at[e, 0 if sy > 0 else 1]
        else:
            src = csend.at[e, i]
            dst = crecv.at[e, o]
        return remote(src, dst, hs.at[e, i], hr.at[e, o], *to)

    def landing(e, side):
        sx, sy = side
        i = SIDES.index(side)
        if sy == 0:
            src = flat.at[e, :, nx - 1 if sx > 0 else 0]
            dst = pads.at[e, :, nx + 1 if sx > 0 else 0, pl.ds(Y0, ny), :]
        elif sx == 0:
            src = ysend.at[e, 1 if sy > 0 else 0]
            dst = yrecv.at[e, 1 if sy > 0 else 0]
        else:
            src = csend.at[e, i]
            dst = crecv.at[e, i]
        return remote(src, dst, hs.at[e, i], hr.at[e, i], dom + sx, bud + sy)

    def pack(e):
        for c in range(3):
            for x in range(nx):
                row = c * nx + x
                ysend[e, 0, row:row + 1, :] = flat[e, c, x, 0:1, :]
                ysend[e, 1, row:row + 1, :] = flat[e, c, x, ny - 1:ny, :]
            for i, (sx, sy) in enumerate(SIDES):
                if sx != 0 and sy != 0:
                    y = ny - 1 if sy > 0 else 0
                    csend[e, i, c:c + 1, :] = flat[e, c, nx - 1 if sx > 0 else 0, y:y + 1, :]

    def send_halo(e):
        for side in SIDES:
            @pl.when(has(side))
            def _(side=side):
                halo_copies(e, 0, side).start()

    def take_halo(e):
        for side in SIDES:
            @pl.when(has(side))
            def _(side=side):
                landing(e, side).wait_recv()
        for c in range(3):
            for x in range(nx):
                row = c * nx + x
                pads[e, c, x + 1, Y0 - 1:Y0, :] = yrecv[e, 0, row:row + 1, :]
                pads[e, c, x + 1, Y0 + ny:Y0 + ny + 1, :] = yrecv[e, 1, row:row + 1, :]
            for i, (sx, sy) in enumerate(SIDES):
                if sx != 0 and sy != 0:
                    y = Y0 + ny if sy > 0 else Y0 - 1
                    pads[e, c, nx + 1 if sx > 0 else 0, y:y + 1, :] = crecv[e, i, c:c + 1, :]

    def end_halo(e):
        for side in SIDES:
            @pl.when(has(side))
            def _(side=side):
                halo_copies(e, 0, side).wait_send()

    lane = lax.broadcasted_iota(jnp.int32, (step, ny, nz), 2)

    def apply(pad, out):
        @pl.loop(0, nx // step)
        def _(j):
            x = j * step
            acc = [[None] * 3 for _ in range(3)]
            for dx in range(3):
                for dy in range(3):
                    for b in range(3):
                        w = pad[b, pl.ds(x + dx, step), Y0 - 1 + dy:Y0 - 1 + dy + ny, :]
                        for dz in range(3):
                            o = (dx * 3 + dy) * 3 + dz
                            for a in range(3):
                                term = cpl[o * 9 + a * 3 + b] * w
                                acc[dz][a] = term if acc[dz][a] is None else acc[dz][a] + term
            for a in range(3):
                before = jnp.where(lane == 0, 0.0, pltpu.roll(acc[0][a], 1, 2))
                after = jnp.where(lane == nz - 1, 0.0, pltpu.roll(acc[2][a], nz - 1, 2))
                out[a, pl.ds(x, step)] = acc[1][a] + before + after

    centre = [cpl[13 * 9 + a * 3 + a] for a in range(3)]

    for a in range(3):
        scaled = jnp.where(me_failed, 0.0, x_in[a] * stiff[...])
        flat[0, a] = scaled
        pads[0, a, 1:nx + 1, Y0:Y0 + ny, :] = scaled
        inv[a] = 1.0 / (stiff[...] * stiff[...] * centre[a])
    pack(0)

    beside_x = jnp.where(dom > 0, 1, 0) + jnp.where(dom < nd - 1, 1, 0)
    beside_y = jnp.where(bud > 0, 1, 0) + jnp.where(bud < nb - 1, 1, 0)
    pl.semaphore_wait(barrier, nb - 1 + nd - 1 + beside_x * beside_y)

    fetch = [[remote(bk.at[w], saved.at[l, w], ss.at[l, w], sr.at[l, w], dom, flip(l))
              for l in range(levels)] for w in range(2)]
    for l in range(levels):
        fetch[1][l].start()
    send_halo(0)
    for l in range(levels):
        fetch[0][l].start()

    keep = [[remote(bsend.at[w], brecv.at[l, w], bs.at[l, w], br.at[l, w], dom, flip(l))
             for l in range(levels)] for w in range(3)]

    def pick(buf, w, a):
        value = buf[0, w, a]
        for l in range(1, levels):
            value = jnp.where(bit_here == l, buf[l, w, a], value)
        return value

    for l in range(levels):
        fetch[1][l].wait_recv()
    for a in range(3):
        p0 = jnp.where(me_failed, pick(saved, 1, a), p_in[a])
        bsend[0, a] = p0
        u0 = p0 * stiff[...]
        flat[1, a] = u0
        pads[1, a, 1:nx + 1, Y0:Y0 + ny, :] = u0
    pack(1)
    send_halo(1)
    for l in range(levels):
        fetch[0][l].wait_recv()
    for a in range(3):
        restored_z = pick(saved, 1, a) - beta[0] * pick(saved, 0, a)
        restored_r = restored_z * (stiff[...] * stiff[...] * centre[a])
        z0 = jnp.where(me_failed, restored_z, inv[a] * r_in[a])
        r0[a] = jnp.where(me_failed, restored_r, r_in[a])
        target[a] = rhs[a] - restored_r
        bsend[1, a] = z0
        a0 = z0 * stiff[...]
        flat[2, a] = a0
        pads[2, a, 1:nx + 1, Y0:Y0 + ny, :] = a0
    pack(2)
    send_halo(2)
    for l in range(levels):
        keep[0][l].start()
    for l in range(levels):
        keep[1][l].start()

    take_halo(1)
    apply(pads.at[1], img.at[0])
    for a in range(3):
        b0 = img[0, a] * (1.0 / jnp.full((1, ny, nz), centre[a], jnp.float32))
        flat[3, a] = b0
        pads[3, a, 1:nx + 1, Y0:Y0 + ny, :] = b0
    pack(3)
    send_halo(3)
    for a in range(3):
        bsend[2, a] = flat[3, a] / stiff[...]
    for l in range(levels):
        keep[2][l].start()

    take_halo(2)
    apply(pads.at[2], img.at[1])
    take_halo(0)
    apply(pads.at[0], img.at[3])
    take_halo(3)
    apply(pads.at[3], img.at[2])

    def dot(*terms):
        total = None
        for a in range(3):
            for v in terms:
                t = v(a)
                total = t if total is None else total + t
        return jnp.sum(jnp.sum(total, axis=0), axis=0, keepdims=True)

    red[...] = jnp.zeros(red.shape, red.dtype)
    red[0:1, :] = dot(lambda a: r0[a] * bsend[1, a])
    red[1:2, :] = dot(lambda a: flat[1, a] * img[0, a])
    red[2:3, :] = dot(lambda a: flat[2, a] * img[0, a])
    red[3:4, :] = dot(lambda a: flat[3, a] * img[0, a])
    red[4:5, :] = dot(lambda a: flat[2, a] * img[1, a])
    red[5:6, :] = dot(lambda a: flat[3, a] * img[1, a])
    red[6:7, :] = dot(lambda a: flat[3, a] * img[2, a])

    first = [remote(red, rrecv.at[j - 1], d1s.at[j - 1], d1r.at[j - 1], lax.rem(dom + j, nd), bud)
             for j in range(1, nd)]
    for c in first:
        c.start()

    centre_value = (HIGH + LOW) / 2.0
    half_width = (HIGH - LOW) / 2.0
    ratio_value = centre_value / half_width
    weight = 1.0 / ratio_value
    for a in range(3):
        t = target[a] - img[3, a] * stiff[...]
        d = inv[a] * t / centre_value
        target[a] = t
        update[a] = d
        solved[a] = d
        padl[a, 1:nx + 1, Y0:Y0 + ny, :] = d * stiff[...]
    for sweep in range(SWEEPS - 1):
        apply(padl, img.at[3])
        weight_next = 1.0 / (2.0 * ratio_value - weight)
        for a in range(3):
            remain = target[a] - img[3, a] * stiff[...]
            d = weight_next * weight * update[a] + (2.0 * weight_next / half_width) * (inv[a] * remain)
            y = solved[a] + d
            update[a] = d
            solved[a] = y
            if sweep < SWEEPS - 2:
                padl[a, 1:nx + 1, Y0:Y0 + ny, :] = y * stiff[...]
        weight = weight_next

    for c in first:
        c.wait_recv()
    total = red[...]
    for j in range(nd - 1):
        total = total + rrecv[j]
    red2[...] = total
    second = [remote(red2, brecv2.at[j - 1], d2s.at[j - 1], d2r.at[j - 1], dom, lax.rem(bud + j, nb))
              for j in range(1, nb)]
    for c in second:
        c.start()
    for w in range(3):
        for l in range(levels):
            keep[w][l].wait_recv()
    for a in range(3):
        b_out[0, a] = pick(brecv, 0, a)
    for c in second:
        c.wait_recv()
    total = red2[...]
    for j in range(nb - 1):
        total = total + brecv2[j]
    sums = jnp.sum(total, axis=1, keepdims=True)
    g0, c0, e0, f0, h0, h1, h2 = [jnp.broadcast_to(sums[j:j + 1], (1, nz)) for j in range(7)]
    alpha0 = g0 / c0
    g1 = g0 - 2.0 * alpha0 * e0 + alpha0 * alpha0 * f0
    beta0 = g1 / g0
    c1 = (
        h0 - 2.0 * alpha0 * h1 + alpha0 * alpha0 * h2
        + 2.0 * beta0 * (e0 - alpha0 * f0) + beta0 * beta0 * c0
    )
    alpha1 = g1 / c1
    alpha0, beta0, alpha1 = alpha0[None], beta0[None], alpha1[None]
    for a in range(3):
        p0 = bsend[0, a]
        p1 = bsend[1, a] - alpha0 * bsend[2, a] + beta0 * p0
        x0 = jnp.where(me_failed, solved[a], x_in[a])
        x_out[a] = x0 + alpha0 * p0 + alpha1 * p1
        t0 = img[0, a]
        q1 = img[1, a] - alpha0 * img[2, a] + beta0 * t0
        r_out[a] = r0[a] - stiff[...] * (alpha0 * t0 + alpha1 * q1)
        b_out[1, a] = (
            pick(brecv, 1, a) - alpha0 * pick(brecv, 2, a) + beta0 * pick(brecv, 0, a)
        )

    for e in range(4):
        end_halo(e)
    for w in range(2):
        for l in range(levels):
            fetch[w][l].wait_send()
    for w in range(3):
        for l in range(levels):
            keep[w][l].wait_send()
    for c in first + second:
        c.wait_send()


def on_device(nd, nb, rhs, stiff, coupling, x_in, r_in, p_in, backup_in, beta, fc, bb):
    levels = nb.bit_length() - 1
    nx, ny, nz = stiff.shape
    f32 = jnp.float32
    rows = -(-3 * nx // 8) * 8
    vmem = pl.BlockSpec(memory_space=pltpu.VMEM)
    smem = pl.BlockSpec(memory_space=pltpu.SMEM)
    field = (3, nx, ny, nz)
    dma = pltpu.SemaphoreType.DMA
    return pl.pallas_call(
        functools.partial(kernel, nd, nb, levels),
        out_shape=(
            jax.ShapeDtypeStruct(field, f32),
            jax.ShapeDtypeStruct(field, f32),
            jax.ShapeDtypeStruct((2,) + field, f32),
        ),
        in_specs=[vmem, vmem, smem, vmem, vmem, vmem, vmem, smem, smem, smem],
        out_specs=(vmem, vmem, vmem),
        scratch_shapes=[
            pltpu.VMEM((4, 3, nx + 2, ny + 2 * Y0, nz), f32),
            pltpu.VMEM((3, nx + 2, ny + 2 * Y0, nz), f32),
            pltpu.VMEM((4,) + field, f32),
            pltpu.VMEM((4, 2, rows, nz), f32),
            pltpu.VMEM((4, 2, rows, nz), f32),
            pltpu.VMEM((4, 8, 8, nz), f32),
            pltpu.VMEM((4, 8, 8, nz), f32),
            pltpu.VMEM((levels, 2) + field, f32),
            pltpu.VMEM((3,) + field, f32),
            pltpu.VMEM((levels, 3) + field, f32),
            pltpu.VMEM(field, f32),
            pltpu.VMEM(field, f32),
            pltpu.VMEM((4,) + field, f32),
            pltpu.VMEM(field, f32),
            pltpu.VMEM(field, f32),
            pltpu.VMEM(field, f32),
            pltpu.VMEM((8, nz), f32),
            pltpu.VMEM((8, nz), f32),
            pltpu.VMEM((nd - 1, 8, nz), f32),
            pltpu.VMEM((nb - 1, 8, nz), f32),
            dma((4, 8)), dma((4, 8)),
            dma((levels, 2)), dma((levels, 2)),
            dma((levels, 3)), dma((levels, 3)),
            dma((nd - 1,)), dma((nd - 1,)),
            dma((nb - 1,)), dma((nb - 1,)),
        ],
        compiler_params=pltpu.CompilerParams(
            collective_id=0, has_side_effects=True, vmem_limit_bytes=40 * 1024 * 1024
        ),
    )(rhs, stiff, coupling.reshape(-1), x_in, r_in, p_in, backup_in, beta, fc, bb)


def solution(mesh):
    nd, nb = mesh.shape["dom"], mesh.shape["bud"]
    placed = (
        P(None, "dom", "bud", None),
        P("dom", "bud", None),
        P(),
        P(None, "dom", "bud", None),
        P(None, "dom", "bud", None),
        P(None, "dom", "bud", None),
        P(None, None, "dom", "bud", None),
        P(),
        P("dom"),
        P("dom"),
    )
    return jax.shard_map(
        functools.partial(on_device, nd, nb),
        mesh=mesh,
        in_specs=placed,
        out_specs=(
            P(None, "dom", "bud", None),
            P(None, "dom", "bud", None),
            P(None, None, "dom", "bud", None),
        ),
        check_vma=False,
    )
```

```python
import functools

import jax
import jax.numpy as jnp
from jax import lax
from jax.experimental import pallas as pl
from jax.experimental.pallas import tpu as pltpu
from jax.sharding import PartitionSpec as P

SWEEPS = 4
LOW = 0.01
HIGH = 1.99
SIDES = [(sx, sy) for sx in (-1, 0, 1) for sy in (-1, 0, 1) if (sx, sy) != (0, 0)]
Y0 = 8


def kernel(
    nd, nb, levels,
    rhs_h, stiff_h, cpl_h, x_h, r_h, p_h, bk, beta, fc, bb,
    x_out, r_out, b_out,
    rhs, stiff, cpl, x_in, r_in, p_in, in_sems,
    pads, padl, flat, ysend, yrecv, csend, crecv, saved, bsend, brecv,
    r0, inv, img, target, solved, update,
    red, red2, rrecv, brecv2,
    hs, hr, ss, sr, bs, br, d1s, d1r, d2s, d2r,
):
    nx, ny, nz = stiff.shape
    step = 2 if nx % 2 == 0 else 1
    dom, bud = lax.axis_index("dom"), lax.axis_index("bud")

    def has(side):
        sx, sy = side
        ok = None
        for cond in (
            ([dom > 0] if sx < 0 else [dom < nd - 1] if sx > 0 else [])
            + ([bud > 0] if sy < 0 else [bud < nb - 1] if sy > 0 else [])
        ):
            ok = cond if ok is None else jnp.logical_and(ok, cond)
        return ok

    def remote(src, dst, send, recv, d, b):
        return pltpu.make_async_remote_copy(
            src_ref=src, dst_ref=dst, send_sem=send, recv_sem=recv,
            device_id={"dom": d, "bud": b}, device_id_type=pl.DeviceIdType.MESH,
        )

    def flip(level):
        stride = 1 << level
        return bud + stride * (1 - 2 * (lax.rem(bud // stride, 2)))

    loads = {}
    for i, (name, src, dst) in enumerate((
        ("cpl", cpl_h, cpl), ("stiff", stiff_h, stiff), ("x", x_h, x_in),
        ("p", p_h, p_in), ("r", r_h, r_in), ("rhs", rhs_h, rhs),
    )):
        loads[name] = pltpu.make_async_copy(src, dst, in_sems.at[i])
        loads[name].start()

    pads[...] = jnp.zeros(pads.shape, pads.dtype)
    padl[...] = jnp.zeros(padl.shape, padl.dtype)
    yrecv[...] = jnp.zeros(yrecv.shape, yrecv.dtype)
    crecv[...] = jnp.zeros(crecv.shape, crecv.dtype)

    barrier = pltpu.get_barrier_semaphore()

    def greet(d, b):
        pl.semaphore_signal(
            barrier, inc=1, device_id={"dom": d, "bud": b},
            device_id_type=pl.DeviceIdType.MESH,
        )

    for j in range(1, nb):
        greet(dom, lax.rem(bud + j, nb))
    for j in range(1, nd):
        greet(lax.rem(dom + j, nd), bud)
    diagonals = [s for s in SIDES if s[0] != 0 and s[1] != 0]
    for side in diagonals:
        @pl.when(has(side))
        def _(side=side):
            greet(dom + side[0], bud + side[1])

    for name in ("cpl", "stiff", "x"):
        loads[name].wait()
    me_failed = jnp.full((1, ny, nz), fc[0], jnp.int32) == bud
    bit_here = jnp.full((1, ny, nz), bb[0], jnp.int32)

    def halo_copies(e, which, side):
        sx, sy = side
        i = SIDES.index(side)
        o = SIDES.index((-sx, -sy))
        to = (dom + sx, bud + sy)
        if sy == 0:
            src = flat.at[e, :, nx - 1 if sx > 0 else 0]
            dst = pads.at[e, :, 0 if sx > 0 else nx + 1, pl.ds(Y0, ny), :]
        elif sx == 0:
            src = ysend.at[e, 1 if sy > 0 else 0]
            dst = yrecv.at[e, 0 if sy > 0 else 1]
        else:
            src = csend.at[e, i]
            dst = crecv.at[e, o]
        return remote(src, dst, hs.at[e, i], hr.at[e, o], *to)

    def landing(e, side):
        sx, sy = side
        i = SIDES.index(side)
        if sy == 0:
            src = flat.at[e, :, nx - 1 if sx > 0 else 0]
            dst = pads.at[e, :, nx + 1 if sx > 0 else 0, pl.ds(Y0, ny), :]
        elif sx == 0:
            src = ysend.at[e, 1 if sy > 0 else 0]
            dst = yrecv.at[e, 1 if sy > 0 else 0]
        else:
            src = csend.at[e, i]
            dst = crecv.at[e, i]
        return remote(src, dst, hs.at[e, i], hr.at[e, i], dom + sx, bud + sy)

    def pack(e):
        for c in range(3):
            for x in range(nx):
                row = c * nx + x
                ysend[e, 0, row:row + 1, :] = flat[e, c, x, 0:1, :]
                ysend[e, 1, row:row + 1, :] = flat[e, c, x, ny - 1:ny, :]
            for i, (sx, sy) in enumerate(SIDES):
                if sx != 0 and sy != 0:
                    y = ny - 1 if sy > 0 else 0
                    csend[e, i, c:c + 1, :] = flat[e, c, nx - 1 if sx > 0 else 0, y:y + 1, :]

    def send_halo(e):
        for side in SIDES:
            @pl.when(has(side))
            def _(side=side):
                halo_copies(e, 0, side).start()

    def take_halo(e):
        for side in SIDES:
            @pl.when(has(side))
            def _(side=side):
                landing(e, side).wait_recv()
        for c in range(3):
            for x in range(nx):
                row = c * nx + x
                pads[e, c, x + 1, Y0 - 1:Y0, :] = yrecv[e, 0, row:row + 1, :]
                pads[e, c, x + 1, Y0 + ny:Y0 + ny + 1, :] = yrecv[e, 1, row:row + 1, :]
            for i, (sx, sy) in enumerate(SIDES):
                if sx != 0 and sy != 0:
                    y = Y0 + ny if sy > 0 else Y0 - 1
                    pads[e, c, nx + 1 if sx > 0 else 0, y:y + 1, :] = crecv[e, i, c:c + 1, :]

    def end_halo(e):
        for side in SIDES:
            @pl.when(has(side))
            def _(side=side):
                halo_copies(e, 0, side).wait_send()

    lane = lax.broadcasted_iota(jnp.int32, (step, ny, nz), 2)

    def apply(pad, out):
        @pl.loop(0, nx // step)
        def _(j):
            x = j * step
            acc = [[None] * 3 for _ in range(3)]
            for dx in range(3):
                for dy in range(3):
                    for b in range(3):
                        w = pad[b, pl.ds(x + dx, step), Y0 - 1 + dy:Y0 - 1 + dy + ny, :]
                        for dz in range(3):
                            o = (dx * 3 + dy) * 3 + dz
                            for a in range(3):
                                term = cpl[a, b, o] * w
                                acc[dz][a] = term if acc[dz][a] is None else acc[dz][a] + term
            for a in range(3):
                before = jnp.where(lane == 0, 0.0, pltpu.roll(acc[0][a], 1, 2))
                after = jnp.where(lane == nz - 1, 0.0, pltpu.roll(acc[2][a], nz - 1, 2))
                out[a, pl.ds(x, step)] = acc[1][a] + before + after

    centre = [cpl[a, a, 13] for a in range(3)]

    for a in range(3):
        scaled = jnp.where(me_failed, 0.0, x_in[a] * stiff[...])
        flat[0, a] = scaled
        pads[0, a, 1:nx + 1, Y0:Y0 + ny, :] = scaled
        inv[a] = 1.0 / (stiff[...] * stiff[...] * centre[a])
    pack(0)

    beside_x = jnp.where(dom > 0, 1, 0) + jnp.where(dom < nd - 1, 1, 0)
    beside_y = jnp.where(bud > 0, 1, 0) + jnp.where(bud < nb - 1, 1, 0)
    pl.semaphore_wait(barrier, nb - 1 + nd - 1 + beside_x * beside_y)

    fetch = [[remote(bk.at[w], saved.at[l, w], ss.at[l, w], sr.at[l, w], dom, flip(l))
              for l in range(levels)] for w in range(2)]
    for l in range(levels):
        fetch[1][l].start()
    send_halo(0)
    for l in range(levels):
        fetch[0][l].start()

    keep = [[remote(bsend.at[w], brecv.at[l, w], bs.at[l, w], br.at[l, w], dom, flip(l))
             for l in range(levels)] for w in range(3)]

    def pick(buf, w, a):
        value = buf[0, w, a]
        for l in range(1, levels):
            value = jnp.where(bit_here == l, buf[l, w, a], value)
        return value

    loads["p"].wait()
    for l in range(levels):
        fetch[1][l].wait_recv()
    for a in range(3):
        p0 = jnp.where(me_failed, pick(saved, 1, a), p_in[a])
        bsend[0, a] = p0
        u0 = p0 * stiff[...]
        flat[1, a] = u0
        pads[1, a, 1:nx + 1, Y0:Y0 + ny, :] = u0
    pack(1)
    send_halo(1)
    for name in ("r", "rhs"):
        loads[name].wait()
    for l in range(levels):
        fetch[0][l].wait_recv()
    for a in range(3):
        restored_z = pick(saved, 1, a) - beta[0] * pick(saved, 0, a)
        restored_r = restored_z * (stiff[...] * stiff[...] * centre[a])
        z0 = jnp.where(me_failed, restored_z, inv[a] * r_in[a])
        r0[a] = jnp.where(me_failed, restored_r, r_in[a])
        target[a] = rhs[a] - restored_r
        bsend[1, a] = z0
        a0 = z0 * stiff[...]
        flat[2, a] = a0
        pads[2, a, 1:nx + 1, Y0:Y0 + ny, :] = a0
    pack(2)
    send_halo(2)

    take_halo(1)
    apply(pads.at[1], img.at[0])
    for a in range(3):
        b0 = img[0, a] * (1.0 / jnp.full((1, ny, nz), centre[a], jnp.float32))
        flat[3, a] = b0
        pads[3, a, 1:nx + 1, Y0:Y0 + ny, :] = b0
    pack(3)
    send_halo(3)
    for a in range(3):
        bsend[2, a] = flat[3, a] / stiff[...]
    for w in range(3):
        for l in range(levels):
            keep[w][l].start()

    take_halo(2)
    apply(pads.at[2], img.at[1])
    take_halo(0)
    apply(pads.at[0], img.at[3])
    take_halo(3)
    apply(pads.at[3], img.at[2])

    def dot(*terms):
        total = None
        for a in range(3):
            for v in terms:
                t = v(a)
                total = t if total is None else total + t
        return jnp.sum(jnp.sum(total, axis=0), axis=0, keepdims=True)

    red[...] = jnp.zeros(red.shape, red.dtype)
    red[0:1, :] = dot(lambda a: r0[a] * bsend[1, a])
    red[1:2, :] = dot(lambda a: flat[1, a] * img[0, a])
    red[2:3, :] = dot(lambda a: flat[2, a] * img[0, a])
    red[3:4, :] = dot(lambda a: flat[3, a] * img[0, a])
    red[4:5, :] = dot(lambda a: flat[2, a] * img[1, a])
    red[5:6, :] = dot(lambda a: flat[3, a] * img[1, a])
    red[6:7, :] = dot(lambda a: flat[3, a] * img[2, a])

    first = [remote(red, rrecv.at[j - 1], d1s.at[j - 1], d1r.at[j - 1], lax.rem(dom + j, nd), bud)
             for j in range(1, nd)]
    for c in first:
        c.start()

    centre_value = (HIGH + LOW) / 2.0
    half_width = (HIGH - LOW) / 2.0
    ratio_value = centre_value / half_width
    weight = 1.0 / ratio_value
    for a in range(3):
        t = target[a] - img[3, a] * stiff[...]
        d = inv[a] * t / centre_value
        target[a] = t
        update[a] = d
        solved[a] = d
        padl[a, 1:nx + 1, Y0:Y0 + ny, :] = d * stiff[...]
    for sweep in range(SWEEPS - 1):
        apply(padl, img.at[3])
        weight_next = 1.0 / (2.0 * ratio_value - weight)
        for a in range(3):
            remain = target[a] - img[3, a] * stiff[...]
            d = weight_next * weight * update[a] + (2.0 * weight_next / half_width) * (inv[a] * remain)
            y = solved[a] + d
            update[a] = d
            solved[a] = y
            if sweep < SWEEPS - 2:
                padl[a, 1:nx + 1, Y0:Y0 + ny, :] = y * stiff[...]
        weight = weight_next

    for c in first:
        c.wait_recv()
    total = red[...]
    for j in range(nd - 1):
        total = total + rrecv[j]
    red2[...] = total
    second = [remote(red2, brecv2.at[j - 1], d2s.at[j - 1], d2r.at[j - 1], dom, lax.rem(bud + j, nb))
              for j in range(1, nb)]
    for c in second:
        c.start()
    for w in range(3):
        for l in range(levels):
            keep[w][l].wait_recv()
    for a in range(3):
        b_out[0, a] = pick(brecv, 0, a)
    for c in second:
        c.wait_recv()
    total = red2[...]
    for j in range(nb - 1):
        total = total + brecv2[j]
    sums = jnp.sum(total, axis=1, keepdims=True)
    g0, c0, e0, f0, h0, h1, h2 = [jnp.broadcast_to(sums[j:j + 1], (1, nz)) for j in range(7)]
    alpha0 = g0 / c0
    g1 = g0 - 2.0 * alpha0 * e0 + alpha0 * alpha0 * f0
    beta0 = g1 / g0
    c1 = (
        h0 - 2.0 * alpha0 * h1 + alpha0 * alpha0 * h2
        + 2.0 * beta0 * (e0 - alpha0 * f0) + beta0 * beta0 * c0
    )
    alpha1 = g1 / c1
    alpha0, beta0, alpha1 = alpha0[None], beta0[None], alpha1[None]
    for a in range(3):
        p0 = bsend[0, a]
        p1 = bsend[1, a] - alpha0 * bsend[2, a] + beta0 * p0
        x0 = jnp.where(me_failed, solved[a], x_in[a])
        x_out[a] = x0 + alpha0 * p0 + alpha1 * p1
        t0 = img[0, a]
        q1 = img[1, a] - alpha0 * img[2, a] + beta0 * t0
        r_out[a] = r0[a] - stiff[...] * (alpha0 * t0 + alpha1 * q1)
        b_out[1, a] = (
            pick(brecv, 1, a) - alpha0 * pick(brecv, 2, a) + beta0 * pick(brecv, 0, a)
        )

    for e in range(4):
        end_halo(e)
    for w in range(2):
        for l in range(levels):
            fetch[w][l].wait_send()
    for w in range(3):
        for l in range(levels):
            keep[w][l].wait_send()
    for c in first + second:
        c.wait_send()


def on_device(nd, nb, rhs, stiff, coupling, x_in, r_in, p_in, backup_in, beta, fc, bb):
    levels = nb.bit_length() - 1
    nx, ny, nz = stiff.shape
    f32 = jnp.float32
    rows = -(-3 * nx // 8) * 8
    vmem = pl.BlockSpec(memory_space=pltpu.VMEM)
    smem = pl.BlockSpec(memory_space=pltpu.SMEM)
    field = (3, nx, ny, nz)
    dma = pltpu.SemaphoreType.DMA
    return pl.pallas_call(
        functools.partial(kernel, nd, nb, levels),
        out_shape=(
            jax.ShapeDtypeStruct(field, f32),
            jax.ShapeDtypeStruct(field, f32),
            jax.ShapeDtypeStruct((2,) + field, f32),
        ),
        in_specs=[pl.BlockSpec(memory_space=pltpu.HBM)] * 7 + [smem] * 3,
        out_specs=(vmem, vmem, vmem),
        scratch_shapes=[
            pltpu.VMEM(field, f32),
            pltpu.VMEM((nx, ny, nz), f32),
            pltpu.SMEM((3, 3, 27), f32),
            pltpu.VMEM(field, f32),
            pltpu.VMEM(field, f32),
            pltpu.VMEM(field, f32),
            dma((6,)),
            pltpu.VMEM((4, 3, nx + 2, ny + 2 * Y0, nz), f32),
            pltpu.VMEM((3, nx + 2, ny + 2 * Y0, nz), f32),
            pltpu.VMEM((4,) + field, f32),
            pltpu.VMEM((4, 2, rows, nz), f32),
            pltpu.VMEM((4, 2, rows, nz), f32),
            pltpu.VMEM((4, 8, 8, nz), f32),
            pltpu.VMEM((4, 8, 8, nz), f32),
            pltpu.VMEM((levels, 2) + field, f32),
            pltpu.VMEM((3,) + field, f32),
            pltpu.VMEM((levels, 3) + field, f32),
            pltpu.VMEM(field, f32),
            pltpu.VMEM(field, f32),
            pltpu.VMEM((4,) + field, f32),
            pltpu.VMEM(field, f32),
            pltpu.VMEM(field, f32),
            pltpu.VMEM(field, f32),
            pltpu.VMEM((8, nz), f32),
            pltpu.VMEM((8, nz), f32),
            pltpu.VMEM((nd - 1, 8, nz), f32),
            pltpu.VMEM((nb - 1, 8, nz), f32),
            dma((4, 8)), dma((4, 8)),
            dma((levels, 2)), dma((levels, 2)),
            dma((levels, 3)), dma((levels, 3)),
            dma((nd - 1,)), dma((nd - 1,)),
            dma((nb - 1,)), dma((nb - 1,)),
        ],
        compiler_params=pltpu.CompilerParams(
            collective_id=0, has_side_effects=True, vmem_limit_bytes=40 * 1024 * 1024
        ),
    )(*[pltpu.with_memory_space_constraint(v, pltpu.HBM) for v in (
        rhs, stiff, jnp.transpose(coupling, (1, 2, 0)), x_in, r_in, p_in, backup_in
    )], beta, fc, bb)


def solution(mesh):
    nd, nb = mesh.shape["dom"], mesh.shape["bud"]
    placed = (
        P(None, "dom", "bud", None),
        P("dom", "bud", None),
        P(),
        P(None, "dom", "bud", None),
        P(None, "dom", "bud", None),
        P(None, "dom", "bud", None),
        P(None, None, "dom", "bud", None),
        P(),
        P("dom"),
        P("dom"),
    )
    return jax.shard_map(
        functools.partial(on_device, nd, nb),
        mesh=mesh,
        in_specs=placed,
        out_specs=(
            P(None, "dom", "bud", None),
            P(None, "dom", "bud", None),
            P(None, None, "dom", "bud", None),
        ),
        check_vma=False,
    )
```

```python
import functools

import jax
import jax.numpy as jnp
from jax import lax
from jax.experimental import pallas as pl
from jax.experimental.pallas import tpu as pltpu
from jax.sharding import PartitionSpec as P

SWEEPS = 4
LOW = 0.01
HIGH = 1.99
SIDES = [(sx, sy) for sx in (-1, 0, 1) for sy in (-1, 0, 1) if (sx, sy) != (0, 0)]
Y0 = 8


def kernel(
    nd, nb, levels,
    rhs_h, stiff_h, cpl_h, x_h, r_h, p_h, bk, beta, fc, bb,
    x_out, r0, bsend, b_out, img, s_out, coef,
    rhs, stiff, cpl, x_in, r_in, p_in, in_sems,
    pads, padl, flat, ysend, yrecv, csend, crecv, saved, brecv,
    inv, img3, target, solved, update,
    red, red1, red2, rrecv, brecv2,
    hs, hr, ss, sr, bs, br, d1s, d1r, d2s, d2r,
):
    nx, ny, nz = stiff.shape
    step = 2 if nx % 2 == 0 else 1
    dom, bud = lax.axis_index("dom"), lax.axis_index("bud")

    def has(side):
        sx, sy = side
        ok = None
        for cond in (
            ([dom > 0] if sx < 0 else [dom < nd - 1] if sx > 0 else [])
            + ([bud > 0] if sy < 0 else [bud < nb - 1] if sy > 0 else [])
        ):
            ok = cond if ok is None else jnp.logical_and(ok, cond)
        return ok

    def remote(src, dst, send, recv, d, b):
        return pltpu.make_async_remote_copy(
            src_ref=src, dst_ref=dst, send_sem=send, recv_sem=recv,
            device_id={"dom": d, "bud": b}, device_id_type=pl.DeviceIdType.MESH,
        )

    def flip(level):
        stride = 1 << level
        return bud + stride * (1 - 2 * (lax.rem(bud // stride, 2)))

    coef[...] = jnp.zeros(coef.shape, coef.dtype)
    loads = {}
    for i, (name, src, dst) in enumerate((
        ("cpl", cpl_h, cpl), ("stiff", stiff_h, stiff), ("x", x_h, x_in),
        ("p", p_h, p_in), ("r", r_h, r_in), ("rhs", rhs_h, rhs),
    )):
        loads[name] = pltpu.make_async_copy(src, dst, in_sems.at[i])
        loads[name].start()

    pads[...] = jnp.zeros(pads.shape, pads.dtype)
    padl[...] = jnp.zeros(padl.shape, padl.dtype)
    yrecv[...] = jnp.zeros(yrecv.shape, yrecv.dtype)
    crecv[...] = jnp.zeros(crecv.shape, crecv.dtype)

    barrier = pltpu.get_barrier_semaphore()

    def greet(d, b):
        pl.semaphore_signal(
            barrier, inc=1, device_id={"dom": d, "bud": b},
            device_id_type=pl.DeviceIdType.MESH,
        )

    for j in range(1, nb):
        greet(dom, lax.rem(bud + j, nb))
    for j in range(1, nd):
        greet(lax.rem(dom + j, nd), bud)
    diagonals = [s for s in SIDES if s[0] != 0 and s[1] != 0]
    for side in diagonals:
        @pl.when(has(side))
        def _(side=side):
            greet(dom + side[0], bud + side[1])

    for name in ("cpl", "stiff", "x"):
        loads[name].wait()
    me_failed = jnp.full((1, ny, nz), fc[0], jnp.int32) == bud
    bit_here = jnp.full((1, ny, nz), bb[0], jnp.int32)

    def halo_copies(e, which, side):
        sx, sy = side
        i = SIDES.index(side)
        o = SIDES.index((-sx, -sy))
        to = (dom + sx, bud + sy)
        if sy == 0:
            src = flat.at[e, :, nx - 1 if sx > 0 else 0]
            dst = pads.at[e, :, 0 if sx > 0 else nx + 1, pl.ds(Y0, ny), :]
        elif sx == 0:
            src = ysend.at[e, 1 if sy > 0 else 0]
            dst = yrecv.at[e, 0 if sy > 0 else 1]
        else:
            src = csend.at[e, i]
            dst = crecv.at[e, o]
        return remote(src, dst, hs.at[e, i], hr.at[e, o], *to)

    def landing(e, side):
        sx, sy = side
        i = SIDES.index(side)
        if sy == 0:
            src = flat.at[e, :, nx - 1 if sx > 0 else 0]
            dst = pads.at[e, :, nx + 1 if sx > 0 else 0, pl.ds(Y0, ny), :]
        elif sx == 0:
            src = ysend.at[e, 1 if sy > 0 else 0]
            dst = yrecv.at[e, 1 if sy > 0 else 0]
        else:
            src = csend.at[e, i]
            dst = crecv.at[e, i]
        return remote(src, dst, hs.at[e, i], hr.at[e, i], dom + sx, bud + sy)

    def pack(e, corners=None):
        for c in range(3):
            for x in range(nx if corners is not True else 0):
                row = c * nx + x
                ysend[e, 0, row:row + 1, :] = flat[e, c, x, 0:1, :]
                ysend[e, 1, row:row + 1, :] = flat[e, c, x, ny - 1:ny, :]
            for i, (sx, sy) in enumerate(SIDES):
                if sx != 0 and sy != 0 and corners is not False:
                    y = ny - 1 if sy > 0 else 0
                    csend[e, i, c:c + 1, :] = flat[e, c, nx - 1 if sx > 0 else 0, y:y + 1, :]

    def send_halo(e, sides=SIDES):
        for side in sides:
            @pl.when(has(side))
            def _(side=side):
                halo_copies(e, 0, side).start()

    def take_halo(e):
        for side in SIDES:
            @pl.when(has(side))
            def _(side=side):
                landing(e, side).wait_recv()
        for c in range(3):
            for x in range(nx):
                row = c * nx + x
                pads[e, c, x + 1, Y0 - 1:Y0, :] = yrecv[e, 0, row:row + 1, :]
                pads[e, c, x + 1, Y0 + ny:Y0 + ny + 1, :] = yrecv[e, 1, row:row + 1, :]
            for i, (sx, sy) in enumerate(SIDES):
                if sx != 0 and sy != 0:
                    y = Y0 + ny if sy > 0 else Y0 - 1
                    pads[e, c, nx + 1 if sx > 0 else 0, y:y + 1, :] = crecv[e, i, c:c + 1, :]

    def end_halo(e):
        for side in SIDES:
            @pl.when(has(side))
            def _(side=side):
                halo_copies(e, 0, side).wait_send()

    lane = lax.broadcasted_iota(jnp.int32, (step, ny, nz), 2)

    def apply(pad, out):
        @pl.loop(0, nx // step)
        def _(j):
            x = j * step
            acc = [[None] * 3 for _ in range(3)]
            for dx in range(3):
                for dy in range(3):
                    for b in range(3):
                        w = pad[b, pl.ds(x + dx, step), Y0 - 1 + dy:Y0 - 1 + dy + ny, :]
                        for dz in range(3):
                            o = (dx * 3 + dy) * 3 + dz
                            for a in range(3):
                                term = cpl[a, b, o] * w
                                acc[dz][a] = term if acc[dz][a] is None else acc[dz][a] + term
            for a in range(3):
                before = jnp.where(lane == 0, 0.0, pltpu.roll(acc[0][a], 1, 2))
                after = jnp.where(lane == nz - 1, 0.0, pltpu.roll(acc[2][a], nz - 1, 2))
                out[a, pl.ds(x, step)] = acc[1][a] + before + after

    centre = [cpl[a, a, 13] for a in range(3)]

    for a in range(3):
        scaled = jnp.where(me_failed, 0.0, x_in[a] * stiff[...])
        flat[0, a] = scaled
        pads[0, a, 1:nx + 1, Y0:Y0 + ny, :] = scaled
        inv[a] = 1.0 / (stiff[...] * stiff[...] * centre[a])
    pack(0)

    beside_x = jnp.where(dom > 0, 1, 0) + jnp.where(dom < nd - 1, 1, 0)
    beside_y = jnp.where(bud > 0, 1, 0) + jnp.where(bud < nb - 1, 1, 0)
    pl.semaphore_wait(barrier, nb - 1 + nd - 1 + beside_x * beside_y)

    pieces = [(0, pl.ds(0, nx)), (1, pl.ds(0, 1)), (1, pl.ds(nx - 1, 1)), (1, pl.ds(1, nx - 2))]
    fetch = [[remote(bk.at[w, :, x], saved.at[l, w, :, x], ss.at[l, i], sr.at[l, i], dom, flip(l))
              for l in range(levels)] for i, (w, x) in enumerate(pieces)]
    for i in (1, 2, 3):
        for l in range(levels):
            fetch[i][l].start()
    send_halo(0)
    for l in range(levels):
        fetch[0][l].start()

    keep = [[remote(bsend.at[w], brecv.at[l, w], bs.at[l, w], br.at[l, w], dom, flip(l))
             for l in range(levels)] for w in range(3)]

    def pick(buf, w, a):
        value = buf[0, w, a]
        for l in range(1, levels):
            value = jnp.where(bit_here == l, buf[l, w, a], value)
        return value

    def start_field(x):
        for a in range(3):
            got = saved[0, 1, a, x]
            for l in range(1, levels):
                got = jnp.where(bit_here == l, saved[l, 1, a, x], got)
            p0 = jnp.where(me_failed, got, p_in[a, x])
            bsend[0, a, x] = p0
            u0 = p0 * stiff[x]
            flat[1, a, x] = u0
            pads[1, a, x.start + 1:x.stop + 1, Y0:Y0 + ny, :] = u0

    loads["p"].wait()
    for i in (1, 2):
        for l in range(levels):
            fetch[i][l].wait_recv()
    start_field(slice(0, 1))
    start_field(slice(nx - 1, nx))
    pack(1, True)
    send_halo(1, [s for s in SIDES if s[0] != 0])
    for l in range(levels):
        fetch[3][l].wait_recv()
    start_field(slice(1, nx - 1))
    pack(1, False)
    send_halo(1, [s for s in SIDES if s[0] == 0])
    for l in range(levels):
        keep[0][l].start()
    for name in ("r", "rhs"):
        loads[name].wait()
    for l in range(levels):
        fetch[0][l].wait_recv()
    for a in range(3):
        restored_z = pick(saved, 1, a) - beta[0] * pick(saved, 0, a)
        restored_r = restored_z * (stiff[...] * stiff[...] * centre[a])
        z0 = jnp.where(me_failed, restored_z, inv[a] * r_in[a])
        r0[a] = jnp.where(me_failed, restored_r, r_in[a])
        target[a] = rhs[a] - restored_r
        bsend[1, a] = z0
        a0 = z0 * stiff[...]
        flat[2, a] = a0
        pads[2, a, 1:nx + 1, Y0:Y0 + ny, :] = a0
    pack(2)
    send_halo(2)

    take_halo(1)
    apply(pads.at[1], img.at[0])
    for a in range(3):
        b0 = img[0, a] * (1.0 / jnp.full((1, ny, nz), centre[a], jnp.float32))
        flat[3, a] = b0
        pads[3, a, 1:nx + 1, Y0:Y0 + ny, :] = b0
    pack(3)
    send_halo(3)
    for a in range(3):
        bsend[2, a] = flat[3, a] / stiff[...]
    for w in (1, 2):
        for l in range(levels):
            keep[w][l].start()

    take_halo(2)
    apply(pads.at[2], img.at[1])
    take_halo(0)
    apply(pads.at[0], img3)
    take_halo(3)
    apply(pads.at[3], img.at[2])

    def dot(*terms):
        total = None
        for a in range(3):
            for v in terms:
                t = v(a)
                total = t if total is None else total + t
        return jnp.sum(jnp.sum(total, axis=0), axis=0, keepdims=True)

    red[...] = jnp.zeros(red.shape, red.dtype)
    red[0:1, :] = dot(lambda a: r0[a] * bsend[1, a])
    red[1:2, :] = dot(lambda a: flat[1, a] * img[0, a])
    red[2:3, :] = dot(lambda a: flat[2, a] * img[0, a])
    red[3:4, :] = dot(lambda a: flat[3, a] * img[0, a])
    red[4:5, :] = dot(lambda a: flat[2, a] * img[1, a])
    red[5:6, :] = dot(lambda a: flat[3, a] * img[1, a])
    red[6:7, :] = dot(lambda a: flat[3, a] * img[2, a])

    rows = lax.broadcasted_iota(jnp.int32, (8, nz), 0)
    diagonal = rows == lax.broadcasted_iota(jnp.int32, (8, nz), 1)
    each = jnp.sum(red[...], axis=1, keepdims=True)
    red1[...] = jnp.sum(jnp.where(diagonal, each, 0.0), axis=0, keepdims=True)
    first = [remote(red1, rrecv.at[j - 1], d1s.at[j - 1], d1r.at[j - 1], lax.rem(dom + j, nd), bud)
             for j in range(1, nd)]
    for c in first:
        c.start()

    centre_value = (HIGH + LOW) / 2.0
    half_width = (HIGH - LOW) / 2.0
    ratio_value = centre_value / half_width
    weight = 1.0 / ratio_value
    for a in range(3):
        t = target[a] - img3[a] * stiff[...]
        d = inv[a] * t / centre_value
        target[a] = t
        update[a] = d
        solved[a] = d
        padl[a, 1:nx + 1, Y0:Y0 + ny, :] = d * stiff[...]
    for sweep in range(SWEEPS - 1):
        apply(padl, img3)
        weight_next = 1.0 / (2.0 * ratio_value - weight)
        for a in range(3):
            remain = target[a] - img3[a] * stiff[...]
            d = weight_next * weight * update[a] + (2.0 * weight_next / half_width) * (inv[a] * remain)
            y = solved[a] + d
            update[a] = d
            solved[a] = y
            if sweep < SWEEPS - 2:
                padl[a, 1:nx + 1, Y0:Y0 + ny, :] = y * stiff[...]
        weight = weight_next

    for c in first:
        c.wait_recv()
    total = red1[...]
    for j in range(nd - 1):
        total = total + rrecv[j]
    red2[...] = total
    second = [remote(red2, brecv2.at[j - 1], d2s.at[j - 1], d2r.at[j - 1], dom, lax.rem(bud + j, nb))
              for j in range(1, nb)]
    for c in second:
        c.start()
    for w in range(3):
        for l in range(levels):
            keep[w][l].wait_recv()
    for c in second:
        c.wait_recv()
    total = red2[...]
    for j in range(nb - 1):
        total = total + brecv2[j]
    sums = jnp.sum(jnp.where(diagonal, jnp.broadcast_to(total, (8, nz)), 0.0), axis=1, keepdims=True)
    g0, c0, e0, f0, h0, h1, h2 = [jnp.broadcast_to(sums[j:j + 1], (1, nz)) for j in range(7)]
    alpha0 = g0 / c0
    g1 = g0 - 2.0 * alpha0 * e0 + alpha0 * alpha0 * f0
    beta0 = g1 / g0
    c1 = (
        h0 - 2.0 * alpha0 * h1 + alpha0 * alpha0 * h2
        + 2.0 * beta0 * (e0 - alpha0 * f0) + beta0 * beta0 * c0
    )
    alpha1 = g1 / c1
    coef[0:1, :] = alpha0
    coef[1:2, :] = beta0
    coef[2:3, :] = alpha1
    for a in range(3):
        x_out[a] = jnp.where(me_failed, solved[a], x_in[a])
        for w in range(3):
            b_out[w, a] = pick(brecv, w, a)

    s_out[...] = stiff[...]
    for e in range(4):
        end_halo(e)
    for i in range(4):
        for l in range(levels):
            fetch[i][l].wait_send()
    for w in range(3):
        for l in range(levels):
            keep[w][l].wait_send()
    for c in first + second:
        c.wait_send()


def finish(x0, r0, own, other, img, stiff, coef, x_out, r_out, b_out, xs, rs, bs, sems):
    copies = [pltpu.make_async_copy(other.at[0], b_out.at[0], sems.at[9])]
    copies[0].start()
    alpha0, beta0, alpha1 = coef[0:1, :], coef[1:2, :], coef[2:3, :]
    alpha0, beta0, alpha1 = alpha0[None], beta0[None], alpha1[None]
    for a in range(3):
        bs[a] = other[1, a] - alpha0 * other[2, a] + beta0 * other[0, a]
        p0 = own[0, a]
        p1 = own[1, a] - alpha0 * own[2, a] + beta0 * p0
        xs[a] = x0[a] + alpha0 * p0 + alpha1 * p1
        t0 = img[0, a]
        q1 = img[1, a] - alpha0 * img[2, a] + beta0 * t0
        rs[a] = r0[a] - stiff[...] * (alpha0 * t0 + alpha1 * q1)
        for i, (src, dst) in enumerate((
            (bs.at[a], b_out.at[1, a]), (xs.at[a], x_out.at[a]), (rs.at[a], r_out.at[a]),
        )):
            copies.append(pltpu.make_async_copy(src, dst, sems.at[a * 3 + i]))
            copies[-1].start()
    for c in copies:
        c.wait()


def on_device(nd, nb, rhs, stiff, coupling, x_in, r_in, p_in, backup_in, beta, fc, bb):
    levels = nb.bit_length() - 1
    nx, ny, nz = stiff.shape
    f32 = jnp.float32
    rows = -(-3 * nx // 8) * 8
    vmem = pl.BlockSpec(memory_space=pltpu.VMEM)
    smem = pl.BlockSpec(memory_space=pltpu.SMEM)
    hbm = pl.BlockSpec(memory_space=pltpu.HBM)
    field = (3, nx, ny, nz)
    dma = pltpu.SemaphoreType.DMA
    parts = pl.pallas_call(
        functools.partial(kernel, nd, nb, levels),
        out_shape=(
            pltpu.VMEM(field, f32),
            pltpu.VMEM(field, f32),
            pltpu.VMEM((3,) + field, f32),
            pltpu.VMEM((3,) + field, f32),
            pltpu.VMEM((3,) + field, f32),
            pltpu.VMEM((nx, ny, nz), f32),
            pltpu.VMEM((8, nz), f32),
        ),
        in_specs=[hbm] * 7 + [smem] * 3,
        out_specs=(vmem,) * 7,
        scratch_shapes=[
            pltpu.VMEM(field, f32),
            pltpu.VMEM((nx, ny, nz), f32),
            pltpu.SMEM((3, 3, 27), f32),
            pltpu.VMEM(field, f32),
            pltpu.VMEM(field, f32),
            pltpu.VMEM(field, f32),
            dma((6,)),
            pltpu.VMEM((4, 3, nx + 2, ny + 2 * Y0, nz), f32),
            pltpu.VMEM((3, nx + 2, ny + 2 * Y0, nz), f32),
            pltpu.VMEM((4,) + field, f32),
            pltpu.VMEM((4, 2, rows, nz), f32),
            pltpu.VMEM((4, 2, rows, nz), f32),
            pltpu.VMEM((4, 8, 8, nz), f32),
            pltpu.VMEM((4, 8, 8, nz), f32),
            pltpu.VMEM((levels, 2) + field, f32),
            pltpu.VMEM((levels, 3) + field, f32),
            pltpu.VMEM(field, f32),
            pltpu.VMEM(field, f32),
            pltpu.VMEM(field, f32),
            pltpu.VMEM(field, f32),
            pltpu.VMEM(field, f32),
            pltpu.VMEM((8, nz), f32),
            pltpu.VMEM((1, nz), f32),
            pltpu.VMEM((1, nz), f32),
            pltpu.VMEM((nd - 1, 1, nz), f32),
            pltpu.VMEM((nb - 1, 1, nz), f32),
            dma((4, 8)), dma((4, 8)),
            dma((levels, 4)), dma((levels, 4)),
            dma((levels, 3)), dma((levels, 3)),
            dma((nd - 1,)), dma((nd - 1,)),
            dma((nb - 1,)), dma((nb - 1,)),
        ],
        compiler_params=pltpu.CompilerParams(
            collective_id=0, has_side_effects=True, vmem_limit_bytes=40 * 1024 * 1024
        ),
    )(*[pltpu.with_memory_space_constraint(v, pltpu.HBM) for v in (
        rhs, stiff, jnp.transpose(coupling, (1, 2, 0)), x_in, r_in, p_in, backup_in
    )], beta, fc, bb)
    return pl.pallas_call(
        finish,
        out_shape=(
            pltpu.HBM(field, f32), pltpu.HBM(field, f32), pltpu.HBM((2,) + field, f32),
        ),
        in_specs=[vmem] * 7,
        out_specs=(hbm, hbm, hbm),
        scratch_shapes=[
            pltpu.VMEM(field, f32), pltpu.VMEM(field, f32), pltpu.VMEM(field, f32), dma((10,)),
        ],
        compiler_params=pltpu.CompilerParams(vmem_limit_bytes=8 * 1024 * 1024),
    )(*parts)


def solution(mesh):
    nd, nb = mesh.shape["dom"], mesh.shape["bud"]
    placed = (
        P(None, "dom", "bud", None),
        P("dom", "bud", None),
        P(),
        P(None, "dom", "bud", None),
        P(None, "dom", "bud", None),
        P(None, "dom", "bud", None),
        P(None, None, "dom", "bud", None),
        P(),
        P("dom"),
        P("dom"),
    )
    return jax.shard_map(
        functools.partial(on_device, nd, nb),
        mesh=mesh,
        in_specs=placed,
        out_specs=(
            P(None, "dom", "bud", None),
            P(None, "dom", "bud", None),
            P(None, None, "dom", "bud", None),
        ),
        check_vma=False,
    )
```

```python
import functools

import jax
import jax.numpy as jnp
from jax import lax
from jax.experimental import pallas as pl
from jax.experimental.pallas import tpu as pltpu
from jax.sharding import PartitionSpec as P

SWEEPS = 4
LOW = 0.01
HIGH = 1.99
SIDES = [(sx, sy) for sx in (-1, 0, 1) for sy in (-1, 0, 1) if (sx, sy) != (0, 0)]
Y0 = 8


def kernel(
    nd, nb, levels,
    rhs_h, stiff_h, cpl_h, x_h, r_h, p_h, bk, beta, fc, bb,
    x_out, r0, bsend, b_out, img, s_out, coef,
    rhs, stiff, cpl, x_in, r_in, p_in, in_sems,
    pads, padl, flat, ysend, yrecv, csend, crecv, saved, brecv,
    inv, img3, target, solved, update,
    red, red1, red2, rrecv, brecv2,
    hs, hr, ss, sr, bs, br, d1s, d1r, d2s, d2r,
):
    nx, ny, nz = stiff.shape
    step = 2 if nx % 2 == 0 else 1
    dom, bud = lax.axis_index("dom"), lax.axis_index("bud")

    def has(side):
        sx, sy = side
        ok = None
        for cond in (
            ([dom > 0] if sx < 0 else [dom < nd - 1] if sx > 0 else [])
            + ([bud > 0] if sy < 0 else [bud < nb - 1] if sy > 0 else [])
        ):
            ok = cond if ok is None else jnp.logical_and(ok, cond)
        return ok

    def remote(src, dst, send, recv, d, b):
        return pltpu.make_async_remote_copy(
            src_ref=src, dst_ref=dst, send_sem=send, recv_sem=recv,
            device_id={"dom": d, "bud": b}, device_id_type=pl.DeviceIdType.MESH,
        )

    def flip(level):
        stride = 1 << level
        return bud + stride * (1 - 2 * (lax.rem(bud // stride, 2)))

    coef[...] = jnp.zeros(coef.shape, coef.dtype)
    loads = {}
    for i, (name, src, dst) in enumerate((
        ("cpl", cpl_h, cpl), ("stiff", stiff_h, stiff), ("x", x_h, x_in),
        ("p", p_h, p_in), ("r", r_h, r_in), ("rhs", rhs_h, rhs),
    )):
        loads[name] = pltpu.make_async_copy(src, dst, in_sems.at[i])
        loads[name].start()

    for pad in [pads.at[e] for e in range(4)] + [padl]:
        face = jnp.zeros((3, ny + 2 * Y0, nz), pad.dtype)
        pad[:, 0] = face
        pad[:, nx + 1] = face
        rim = jnp.zeros((3, nx, Y0, nz), pad.dtype)
        pad[:, 1:nx + 1, 0:Y0, :] = rim
        pad[:, 1:nx + 1, Y0 + ny:ny + 2 * Y0, :] = rim
    yrecv[...] = jnp.zeros(yrecv.shape, yrecv.dtype)
    crecv[...] = jnp.zeros(crecv.shape, crecv.dtype)

    barrier = pltpu.get_barrier_semaphore()

    def greet(d, b):
        pl.semaphore_signal(
            barrier, inc=1, device_id={"dom": d, "bud": b},
            device_id_type=pl.DeviceIdType.MESH,
        )

    for j in range(1, nb):
        greet(dom, lax.rem(bud + j, nb))
    for j in range(1, nd):
        greet(lax.rem(dom + j, nd), bud)
    diagonals = [s for s in SIDES if s[0] != 0 and s[1] != 0]
    for side in diagonals:
        @pl.when(has(side))
        def _(side=side):
            greet(dom + side[0], bud + side[1])

    for name in ("cpl", "stiff", "x"):
        loads[name].wait()
    me_failed = jnp.full((1, ny, nz), fc[0], jnp.int32) == bud
    bit_here = jnp.full((1, ny, nz), bb[0], jnp.int32)

    def halo_copies(e, which, side):
        sx, sy = side
        i = SIDES.index(side)
        o = SIDES.index((-sx, -sy))
        to = (dom + sx, bud + sy)
        if sy == 0:
            src = flat.at[e, :, nx - 1 if sx > 0 else 0]
            dst = pads.at[e, :, 0 if sx > 0 else nx + 1, pl.ds(Y0, ny), :]
        elif sx == 0:
            src = ysend.at[e, 1 if sy > 0 else 0]
            dst = yrecv.at[e, 0 if sy > 0 else 1]
        else:
            src = csend.at[e, i]
            dst = crecv.at[e, o]
        return remote(src, dst, hs.at[e, i], hr.at[e, o], *to)

    def landing(e, side):
        sx, sy = side
        i = SIDES.index(side)
        if sy == 0:
            src = flat.at[e, :, nx - 1 if sx > 0 else 0]
            dst = pads.at[e, :, nx + 1 if sx > 0 else 0, pl.ds(Y0, ny), :]
        elif sx == 0:
            src = ysend.at[e, 1 if sy > 0 else 0]
            dst = yrecv.at[e, 1 if sy > 0 else 0]
        else:
            src = csend.at[e, i]
            dst = crecv.at[e, i]
        return remote(src, dst, hs.at[e, i], hr.at[e, i], dom + sx, bud + sy)

    def pack(e, corners=None):
        for c in range(3):
            for x in range(nx if corners is not True else 0):
                row = c * nx + x
                ysend[e, 0, row:row + 1, :] = flat[e, c, x, 0:1, :]
                ysend[e, 1, row:row + 1, :] = flat[e, c, x, ny - 1:ny, :]
            for i, (sx, sy) in enumerate(SIDES):
                if sx != 0 and sy != 0 and corners is not False:
                    y = ny - 1 if sy > 0 else 0
                    csend[e, i, c:c + 1, :] = flat[e, c, nx - 1 if sx > 0 else 0, y:y + 1, :]

    def send_halo(e, sides=SIDES):
        for side in sides:
            @pl.when(has(side))
            def _(side=side):
                halo_copies(e, 0, side).start()

    def take_halo(e):
        for side in SIDES:
            @pl.when(has(side))
            def _(side=side):
                landing(e, side).wait_recv()
        for c in range(3):
            for x in range(nx):
                row = c * nx + x
                pads[e, c, x + 1, Y0 - 1:Y0, :] = yrecv[e, 0, row:row + 1, :]
                pads[e, c, x + 1, Y0 + ny:Y0 + ny + 1, :] = yrecv[e, 1, row:row + 1, :]
            for i, (sx, sy) in enumerate(SIDES):
                if sx != 0 and sy != 0:
                    y = Y0 + ny if sy > 0 else Y0 - 1
                    pads[e, c, nx + 1 if sx > 0 else 0, y:y + 1, :] = crecv[e, i, c:c + 1, :]

    def end_halo(e):
        for side in SIDES:
            @pl.when(has(side))
            def _(side=side):
                halo_copies(e, 0, side).wait_send()

    lane = lax.broadcasted_iota(jnp.int32, (step, ny, nz), 2)

    def apply(pad, out):
        @pl.loop(0, nx // step)
        def _(j):
            x = j * step
            acc = [[None] * 3 for _ in range(3)]
            for dx in range(3):
                for dy in range(3):
                    for b in range(3):
                        w = pad[b, pl.ds(x + dx, step), Y0 - 1 + dy:Y0 - 1 + dy + ny, :]
                        for dz in range(3):
                            o = (dx * 3 + dy) * 3 + dz
                            for a in range(3):
                                term = cpl[a, b, o] * w
                                acc[dz][a] = term if acc[dz][a] is None else acc[dz][a] + term
            for a in range(3):
                before = jnp.where(lane == 0, 0.0, pltpu.roll(acc[0][a], 1, 2))
                after = jnp.where(lane == nz - 1, 0.0, pltpu.roll(acc[2][a], nz - 1, 2))
                out[a, pl.ds(x, step)] = acc[1][a] + before + after

    centre = [cpl[a, a, 13] for a in range(3)]

    for a in range(3):
        scaled = jnp.where(me_failed, 0.0, x_in[a] * stiff[...])
        flat[0, a] = scaled
        pads[0, a, 1:nx + 1, Y0:Y0 + ny, :] = scaled
        inv[a] = 1.0 / (stiff[...] * stiff[...] * centre[a])
    pack(0)

    beside_x = jnp.where(dom > 0, 1, 0) + jnp.where(dom < nd - 1, 1, 0)
    beside_y = jnp.where(bud > 0, 1, 0) + jnp.where(bud < nb - 1, 1, 0)
    pl.semaphore_wait(barrier, nb - 1 + nd - 1 + beside_x * beside_y)

    pieces = [(0, pl.ds(0, nx)), (1, pl.ds(0, 1)), (1, pl.ds(nx - 1, 1)), (1, pl.ds(1, nx - 2))]
    fetch = [[remote(bk.at[w, :, x], saved.at[l, w, :, x], ss.at[l, i], sr.at[l, i], dom, flip(l))
              for l in range(levels)] for i, (w, x) in enumerate(pieces)]
    for i in (1, 2, 3):
        for l in range(levels):
            fetch[i][l].start()
    send_halo(0)
    for l in range(levels):
        fetch[0][l].start()

    keep = [[remote(bsend.at[w], brecv.at[l, w], bs.at[l, w], br.at[l, w], dom, flip(l))
             for l in range(levels)] for w in range(3)]

    def pick(buf, w, a):
        value = buf[0, w, a]
        for l in range(1, levels):
            value = jnp.where(bit_here == l, buf[l, w, a], value)
        return value

    def start_field(x):
        for a in range(3):
            got = saved[0, 1, a, x]
            for l in range(1, levels):
                got = jnp.where(bit_here == l, saved[l, 1, a, x], got)
            p0 = jnp.where(me_failed, got, p_in[a, x])
            bsend[0, a, x] = p0
            u0 = p0 * stiff[x]
            flat[1, a, x] = u0
            pads[1, a, x.start + 1:x.stop + 1, Y0:Y0 + ny, :] = u0

    loads["p"].wait()
    for i in (1, 2):
        for l in range(levels):
            fetch[i][l].wait_recv()
    start_field(slice(0, 1))
    start_field(slice(nx - 1, nx))
    pack(1, True)
    send_halo(1, [s for s in SIDES if s[0] != 0])
    for l in range(levels):
        fetch[3][l].wait_recv()
    start_field(slice(1, nx - 1))
    pack(1, False)
    send_halo(1, [s for s in SIDES if s[0] == 0])
    for l in range(levels):
        keep[0][l].start()
    for name in ("r", "rhs"):
        loads[name].wait()
    for l in range(levels):
        fetch[0][l].wait_recv()
    for a in range(3):
        restored_z = pick(saved, 1, a) - beta[0] * pick(saved, 0, a)
        restored_r = restored_z * (stiff[...] * stiff[...] * centre[a])
        z0 = jnp.where(me_failed, restored_z, inv[a] * r_in[a])
        r0[a] = jnp.where(me_failed, restored_r, r_in[a])
        target[a] = rhs[a] - restored_r
        bsend[1, a] = z0
        a0 = z0 * stiff[...]
        flat[2, a] = a0
        pads[2, a, 1:nx + 1, Y0:Y0 + ny, :] = a0
    pack(2)
    send_halo(2)

    take_halo(1)
    apply(pads.at[1], img.at[0])
    for a in range(3):
        b0 = img[0, a] * (1.0 / jnp.full((1, ny, nz), centre[a], jnp.float32))
        flat[3, a] = b0
        pads[3, a, 1:nx + 1, Y0:Y0 + ny, :] = b0
    pack(3)
    send_halo(3)
    for a in range(3):
        bsend[2, a] = flat[3, a] / stiff[...]
    for w in (1, 2):
        for l in range(levels):
            keep[w][l].start()

    take_halo(2)
    apply(pads.at[2], img.at[1])
    take_halo(0)
    apply(pads.at[0], img3)
    def dot(*terms):
        total = None
        for a in range(3):
            for v in terms:
                t = v(a)
                total = t if total is None else total + t
        return jnp.sum(jnp.sum(total, axis=0), axis=0, keepdims=True)

    red[...] = jnp.zeros(red.shape, red.dtype)
    red[0:1, :] = dot(lambda a: r0[a] * bsend[1, a])
    red[1:2, :] = dot(lambda a: flat[1, a] * img[0, a])
    red[2:3, :] = dot(lambda a: flat[2, a] * img[0, a])
    red[3:4, :] = dot(lambda a: flat[3, a] * img[0, a])
    red[4:5, :] = dot(lambda a: flat[2, a] * img[1, a])
    red[5:6, :] = dot(lambda a: flat[3, a] * img[1, a])
    take_halo(3)
    apply(pads.at[3], img.at[2])
    red[6:7, :] = dot(lambda a: flat[3, a] * img[2, a])

    rows = lax.broadcasted_iota(jnp.int32, (8, nz), 0)
    diagonal = rows == lax.broadcasted_iota(jnp.int32, (8, nz), 1)
    each = jnp.sum(red[...], axis=1, keepdims=True)
    red1[...] = jnp.sum(jnp.where(diagonal, each, 0.0), axis=0, keepdims=True)
    first = [remote(red1, rrecv.at[j - 1], d1s.at[j - 1], d1r.at[j - 1], lax.rem(dom + j, nd), bud)
             for j in range(1, nd)]
    for c in first:
        c.start()

    centre_value = (HIGH + LOW) / 2.0
    half_width = (HIGH - LOW) / 2.0
    ratio_value = centre_value / half_width
    weight = 1.0 / ratio_value
    for a in range(3):
        t = target[a] - img3[a] * stiff[...]
        d = inv[a] * t / centre_value
        target[a] = t
        update[a] = d
        solved[a] = d
        padl[a, 1:nx + 1, Y0:Y0 + ny, :] = d * stiff[...]
    for sweep in range(SWEEPS - 1):
        apply(padl, img3)
        weight_next = 1.0 / (2.0 * ratio_value - weight)
        for a in range(3):
            remain = target[a] - img3[a] * stiff[...]
            d = weight_next * weight * update[a] + (2.0 * weight_next / half_width) * (inv[a] * remain)
            y = solved[a] + d
            update[a] = d
            solved[a] = y
            if sweep < SWEEPS - 2:
                padl[a, 1:nx + 1, Y0:Y0 + ny, :] = y * stiff[...]
        weight = weight_next

    for c in first:
        c.wait_recv()
    total = red1[...]
    for j in range(nd - 1):
        total = total + rrecv[j]
    red2[...] = total
    second = [remote(red2, brecv2.at[j - 1], d2s.at[j - 1], d2r.at[j - 1], dom, lax.rem(bud + j, nb))
              for j in range(1, nb)]
    for c in second:
        c.start()
    for w in range(3):
        for l in range(levels):
            keep[w][l].wait_recv()
    for a in range(3):
        x_out[a] = jnp.where(me_failed, solved[a], x_in[a])
        for w in range(3):
            b_out[w, a] = pick(brecv, w, a)
    s_out[...] = stiff[...]
    for e in range(4):
        end_halo(e)
    for c in second:
        c.wait_recv()
    total = red2[...]
    for j in range(nb - 1):
        total = total + brecv2[j]
    sums = jnp.sum(jnp.where(diagonal, jnp.broadcast_to(total, (8, nz)), 0.0), axis=1, keepdims=True)
    g0, c0, e0, f0, h0, h1, h2 = [jnp.broadcast_to(sums[j:j + 1], (1, nz)) for j in range(7)]
    alpha0 = g0 / c0
    g1 = g0 - 2.0 * alpha0 * e0 + alpha0 * alpha0 * f0
    beta0 = g1 / g0
    c1 = (
        h0 - 2.0 * alpha0 * h1 + alpha0 * alpha0 * h2
        + 2.0 * beta0 * (e0 - alpha0 * f0) + beta0 * beta0 * c0
    )
    alpha1 = g1 / c1
    coef[0:1, :] = alpha0
    coef[1:2, :] = beta0
    coef[2:3, :] = alpha1

    for i in range(4):
        for l in range(levels):
            fetch[i][l].wait_send()
    for w in range(3):
        for l in range(levels):
            keep[w][l].wait_send()
    for c in first + second:
        c.wait_send()


def finish(x0, r0, own, other, img, stiff, coef, x_out, r_out, b_out, xs, rs, bs, sems):
    copies = [pltpu.make_async_copy(other.at[0], b_out.at[0], sems.at[9])]
    copies[0].start()
    alpha0, beta0, alpha1 = coef[0:1, :], coef[1:2, :], coef[2:3, :]
    alpha0, beta0, alpha1 = alpha0[None], beta0[None], alpha1[None]
    for a in range(3):
        bs[a] = other[1, a] - alpha0 * other[2, a] + beta0 * other[0, a]
        p0 = own[0, a]
        p1 = own[1, a] - alpha0 * own[2, a] + beta0 * p0
        xs[a] = x0[a] + alpha0 * p0 + alpha1 * p1
        t0 = img[0, a]
        q1 = img[1, a] - alpha0 * img[2, a] + beta0 * t0
        rs[a] = r0[a] - stiff[...] * (alpha0 * t0 + alpha1 * q1)
        for i, (src, dst) in enumerate((
            (bs.at[a], b_out.at[1, a]), (xs.at[a], x_out.at[a]), (rs.at[a], r_out.at[a]),
        )):
            copies.append(pltpu.make_async_copy(src, dst, sems.at[a * 3 + i]))
            copies[-1].start()
    for c in copies:
        c.wait()


def on_device(nd, nb, rhs, stiff, coupling, x_in, r_in, p_in, backup_in, beta, fc, bb):
    levels = nb.bit_length() - 1
    nx, ny, nz = stiff.shape
    f32 = jnp.float32
    rows = -(-3 * nx // 8) * 8
    vmem = pl.BlockSpec(memory_space=pltpu.VMEM)
    smem = pl.BlockSpec(memory_space=pltpu.SMEM)
    hbm = pl.BlockSpec(memory_space=pltpu.HBM)
    field = (3, nx, ny, nz)
    dma = pltpu.SemaphoreType.DMA
    parts = pl.pallas_call(
        functools.partial(kernel, nd, nb, levels),
        out_shape=(
            pltpu.VMEM(field, f32),
            pltpu.VMEM(field, f32),
            pltpu.VMEM((3,) + field, f32),
            pltpu.VMEM((3,) + field, f32),
            pltpu.VMEM((3,) + field, f32),
            pltpu.VMEM((nx, ny, nz), f32),
            pltpu.VMEM((8, nz), f32),
        ),
        in_specs=[hbm] * 7 + [smem] * 3,
        out_specs=(vmem,) * 7,
        scratch_shapes=[
            pltpu.VMEM(field, f32),
            pltpu.VMEM((nx, ny, nz), f32),
            pltpu.SMEM((3, 3, 27), f32),
            pltpu.VMEM(field, f32),
            pltpu.VMEM(field, f32),
            pltpu.VMEM(field, f32),
            dma((6,)),
            pltpu.VMEM((4, 3, nx + 2, ny + 2 * Y0, nz), f32),
            pltpu.VMEM((3, nx + 2, ny + 2 * Y0, nz), f32),
            pltpu.VMEM((4,) + field, f32),
            pltpu.VMEM((4, 2, rows, nz), f32),
            pltpu.VMEM((4, 2, rows, nz), f32),
            pltpu.VMEM((4, 8, 8, nz), f32),
            pltpu.VMEM((4, 8, 8, nz), f32),
            pltpu.VMEM((levels, 2) + field, f32),
            pltpu.VMEM((levels, 3) + field, f32),
            pltpu.VMEM(field, f32),
            pltpu.VMEM(field, f32),
            pltpu.VMEM(field, f32),
            pltpu.VMEM(field, f32),
            pltpu.VMEM(field, f32),
            pltpu.VMEM((8, nz), f32),
            pltpu.VMEM((1, nz), f32),
            pltpu.VMEM((1, nz), f32),
            pltpu.VMEM((nd - 1, 1, nz), f32),
            pltpu.VMEM((nb - 1, 1, nz), f32),
            dma((4, 8)), dma((4, 8)),
            dma((levels, 4)), dma((levels, 4)),
            dma((levels, 3)), dma((levels, 3)),
            dma((nd - 1,)), dma((nd - 1,)),
            dma((nb - 1,)), dma((nb - 1,)),
        ],
        compiler_params=pltpu.CompilerParams(
            collective_id=0, has_side_effects=True, vmem_limit_bytes=40 * 1024 * 1024
        ),
    )(*[pltpu.with_memory_space_constraint(v, pltpu.HBM) for v in (
        rhs, stiff, jnp.transpose(coupling, (1, 2, 0)), x_in, r_in, p_in, backup_in
    )], beta, fc, bb)
    return pl.pallas_call(
        finish,
        out_shape=(
            pltpu.HBM(field, f32), pltpu.HBM(field, f32), pltpu.HBM((2,) + field, f32),
        ),
        in_specs=[vmem] * 7,
        out_specs=(hbm, hbm, hbm),
        scratch_shapes=[
            pltpu.VMEM(field, f32), pltpu.VMEM(field, f32), pltpu.VMEM(field, f32), dma((10,)),
        ],
        compiler_params=pltpu.CompilerParams(vmem_limit_bytes=8 * 1024 * 1024),
    )(*parts)


def solution(mesh):
    nd, nb = mesh.shape["dom"], mesh.shape["bud"]
    placed = (
        P(None, "dom", "bud", None),
        P("dom", "bud", None),
        P(),
        P(None, "dom", "bud", None),
        P(None, "dom", "bud", None),
        P(None, "dom", "bud", None),
        P(None, None, "dom", "bud", None),
        P(),
        P("dom"),
        P("dom"),
    )
    return jax.shard_map(
        functools.partial(on_device, nd, nb),
        mesh=mesh,
        in_specs=placed,
        out_specs=(
            P(None, "dom", "bud", None),
            P(None, "dom", "bud", None),
            P(None, None, "dom", "bud", None),
        ),
        check_vma=False,
    )
```
